32 devices in a mesh: rep: 16 (over z, x, core), shard: 2 (over y).
Axes of the slice: x: 2, y: 2, z: 4, core: 2. Of those that a mesh axis runs over, the one named last changes fastest.
Arguments:
- tokens: bfloat16 [4096, 1024], P(('rep', 'shard')), may hold values from -6 to 6
- lengths: int32 [32], P(('rep', 'shard')), may hold values from 32 to 128, as said below
- qkv_weight: bfloat16 [1024, 3072], P('shard'), may hold values from -0.1875 to 0.1875
- query_bias: bfloat16 [1024], P('shard'), may hold values from -3 to 3
- value_bias: bfloat16 [1024], P('shard'), may hold values from -3 to 3
- proj_weight: bfloat16 [1024, 1024], P('shard'), may hold values from -0.5 to 0.5
- proj_bias: bfloat16 [1024], P('shard'), may hold values from -3 to 3
- attn_gain: bfloat16 [1024], P('shard'), may hold values from 0.5 to 1.5
- attn_shift: bfloat16 [1024], P('shard'), may hold values from -3 to 3
- up_weight: bfloat16 [1024, 4096], P('shard'), may hold values from -0.1875 to 0.1875
- up_bias: bfloat16 [4096], P('shard'), may hold values from -3 to 3
- down_weight: bfloat16 [4096, 1024], P('shard'), may hold values from -0.09375 to 0.09375
- down_bias: bfloat16 [1024], P('shard'), may hold values from -3 to 3
- ffn_gain: bfloat16 [1024], P('shard'), may hold values from 0.5 to 1.5
- ffn_shift: bfloat16 [1024], P('shard'), may hold values from -3 to 3
- cotangent: bfloat16 [4096, 1024], P(('rep', 'shard')), may hold values from -6 to 6
Outputs:
- layer_output: bfloat16 [4096, 1024], P(('rep', 'shard'))
- grad_tokens: bfloat16 [4096, 1024], P(('rep', 'shard'))
- grad_qkv_weight: float32 [1024, 3072], P('shard')
- grad_query_bias: float32 [1024], P('shard')
- grad_value_bias: float32 [1024], P('shard')
- grad_proj_weight: float32 [1024, 1024], P('shard')
- grad_proj_bias: float32 [1024], P('shard')
- grad_attn_gain: float32 [1024], P('shard')
- grad_attn_shift: float32 [1024], P('shard')
- grad_up_weight: float32 [1024, 4096], P('shard')
- grad_up_bias: float32 [4096], P('shard')
- grad_down_weight: float32 [4096, 1024], P('shard')
- grad_down_bias: float32 [1024], P('shard')
- grad_ffn_gain: float32 [1024], P('shard')
- grad_ffn_shift: float32 [1024], P('shard')
The draws below stay inside these ranges and needn't reach their ends.
Inputs may be any that keep to these rules, and one draw needn't show every extreme that they name: `lengths`: every sequence has at least one quarter of its 128 tokens valid; some sequence is whole and some has exactly 32 valid tokens.
All inputs are finite; a program needn't handle non-finite values.
Results may differ from the reference program's by a relative error of at most 0.018.
Values may be sent and summed in bfloat16 or wider, within the bound.
No kernel may reach another device: no remote copies, remote signals or barrier semaphores. Data moves between devices by JAX's collectives and lax.ppermute only.
A program may use at most 192 MiB of HBM per device.

```python
import math
import jax
import jax.numpy as jnp
from jax import lax

D = 1024
HEADS = 16
HEAD_DIM = 64
FF = 4096
LEN = 128
SEQS = 32
TOKENS = 4096


def draw_lengths(key, part):
    first, second = jax.random.split(jax.random.fold_in(key, 11))
    drawn = jax.random.randint(first, (SEQS,), LEN // 4, LEN + 1, dtype=jnp.int32)
    spot = jax.random.randint(second, (), 0, SEQS, dtype=jnp.int32)
    places = jnp.arange(SEQS, dtype=jnp.int32)
    drawn = jnp.where(places == spot, LEN, drawn)
    drawn = jnp.where(places == (spot + 1) % SEQS, LEN // 4, drawn)
    return drawn.astype(jnp.int32)


def raised(result, own_key, source, target, blocks, factor):
    owner, partner = [(jnp.arange(result.shape[dim]) // (result.shape[dim] // blocks)).reshape([-1 if axis == dim else 1 for axis in range(result.ndim)]) for dim in (source, target)]
    chosen = jax.random.permutation(own_key, blocks)[partner]
    strong = (owner == chosen) | (owner == (partner + blocks // 2) % blocks)
    return jnp.where(strong, factor * result, result)


def level_of(stream_key, extent, pieces, low, high):
    level = 1.0
    for dim, shards_of in pieces:
        heights = jax.random.uniform(jax.random.fold_in(jax.random.fold_in(stream_key, 6), dim), (shards_of,), jnp.float32, low / len(pieces), high / len(pieces))
        level = level * jnp.repeat(jnp.exp(heights), extent[dim] // shards_of).reshape((-1,) + (1,) * (len(extent) - 1 - dim))
    return level


def noise(rng, extent, spread, limit, pieces=(), kind=jnp.bfloat16):
    level = level_of(rng, extent, pieces, -0.22, 0.18) if pieces else 1.0
    values = jax.random.normal(rng, extent, jnp.float32) * spread * level
    return jnp.minimum(jnp.maximum(values, -limit), limit).astype(kind)


def gaussian_with(stream_key, shape, scale, most, cuts, heavy, kind=jnp.bfloat16):
    result = scale * jax.random.normal(stream_key, shape, jnp.float32)
    if cuts:
        result = result * level_of(stream_key, shape, cuts, -0.22, 0.18)
    return jnp.clip(raised(result, jax.random.fold_in(stream_key, 3), *heavy), -most, most).astype(kind)


def setup_inputs(seed: int = 0) -> dict:
    seeds = jax.random.split(jax.random.key(seed), 17)
    return {
        "tokens": noise(seeds[0], (TOKENS, D), 1.0, 6.0, ((0, 32),)),
        "lengths": draw_lengths(jax.random.fold_in(seeds[16], 71), 0),
        "qkv_weight": noise(seeds[2], (D, 3 * D), D ** -0.5, 0.1875, ((0, 2),)),
        "query_bias": noise(seeds[3], (D,), 0.5, 3.0, ((0, 2),)),
        "value_bias": noise(seeds[4], (D,), 0.5, 3.0, ((0, 2),)),
        "proj_weight": noise(seeds[5], (D, D), (D * 16 // LEN) ** -0.5, 0.5, ((0, 2),)),
        "proj_bias": noise(seeds[6], (D,), 0.5, 3.0, ((0, 2),)),
        "attn_gain": jnp.clip(1.0 + 0.1 * jax.random.normal(seeds[7], (D,), jnp.float32), 0.5, 1.5).astype(jnp.bfloat16),
        "attn_shift": noise(seeds[8], (D,), 0.5, 3.0, ((0, 2),)),
        "up_weight": noise(seeds[9], (D, FF), D ** -0.5, 0.1875, ((0, 2),)),
        "up_bias": noise(seeds[10], (FF,), 0.5, 3.0, ((0, 2),)),
        "down_weight": noise(seeds[11], (FF, D), FF ** -0.5, 0.09375, ((0, 2),)),
        "down_bias": noise(seeds[12], (D,), 0.5, 3.0, ((0, 2),)),
        "ffn_gain": jnp.clip(1.0 + 0.1 * jax.random.normal(seeds[13], (D,), jnp.float32), 0.5, 1.5).astype(jnp.bfloat16),
        "ffn_shift": noise(seeds[14], (D,), 0.5, 3.0, ((0, 2),)),
        "cotangent": gaussian_with(seeds[15], (TOKENS, D), 1.0, 6.0, ((0, 32),), (0, 1, 32, 2.75)),
    }


EPSILON = 1e-05
SQRT_HALF = 0.7071067811865476
INV_ROOT_TAU = 0.3989422804014327

def gelu_value(pre_act):
    return 0.5 * pre_act * (1.0 + lax.erf(pre_act * SQRT_HALF))

def gelu_slope(pre_act):
    return 0.5 * (1.0 + lax.erf(pre_act * SQRT_HALF)) + pre_act * INV_ROOT_TAU * jnp.exp(-0.5 * pre_act * pre_act)

def layer_norm(hidden):
    centred = hidden - lax.optimization_barrier(jnp.mean(hidden, axis=-1, keepdims=True))
    inverse = lax.rsqrt(lax.optimization_barrier(jnp.mean(centred * centred, axis=-1, keepdims=True)) + EPSILON)
    return (centred * inverse, inverse)

def norm_backward(upstream, normed, inverse, gain):
    scaled = upstream * gain
    return inverse * (scaled - lax.optimization_barrier(jnp.mean(scaled, axis=-1, keepdims=True)) - normed * lax.optimization_barrier(jnp.mean(scaled * normed, axis=-1, keepdims=True)))

def batched(form, former, latter):
    return jnp.einsum(form, former.astype(jnp.float32), latter.astype(jnp.float32))

def split_heads(matrix):
    return matrix.reshape(matrix.shape[0] // LEN, LEN, HEADS, HEAD_DIM)

def merge_heads(tensor):
    return tensor.reshape(tensor.shape[0] * LEN, HEADS * HEAD_DIM)

def score_block(query_rows, key_rows, lengths):
    scores = batched('sqhd,skhd->shqk', split_heads(query_rows), split_heads(key_rows)) * HEAD_DIM ** (-0.5)
    positions = jnp.arange(LEN, dtype=jnp.int32)
    usable = (positions[None, :] < lengths[:, None])[:, None, None, :]
    return (scores, usable)

def layer_pass(tokens, lengths, cotangent, params):
    qkv_weight, query_bias, value_bias, proj_weight, proj_bias, attn_gain, attn_shift, up_weight, up_bias, down_weight, down_bias, ffn_gain, ffn_shift = params
    model_width = tokens.shape[1]
    project = jnp.dot(tokens, qkv_weight, preferred_element_type=jnp.float32)
    query_rows = (project[:, :model_width] + query_bias.astype(jnp.float32)).astype(jnp.bfloat16)
    key_rows = project[:, model_width:2 * model_width].astype(jnp.bfloat16)
    value_rows = (project[:, 2 * model_width:] + value_bias.astype(jnp.float32)).astype(jnp.bfloat16)
    scores, usable = score_block(query_rows, key_rows, lengths)
    log_total = jnp.log(lax.optimization_barrier(jnp.sum(jnp.where(usable, jnp.exp(scores), 0.0), axis=-1, keepdims=True)))
    exact = jnp.where(usable, jnp.exp(scores - log_total), 0.0)
    shares = exact.astype(jnp.bfloat16)
    context = merge_heads(batched('shqk,skhd->sqhd', shares, split_heads(value_rows))).astype(jnp.bfloat16)
    attn_sum = tokens.astype(jnp.float32) + jnp.dot(context, proj_weight, preferred_element_type=jnp.float32) + proj_bias.astype(jnp.float32)
    normed_one, inverse_one = layer_norm(attn_sum)
    mid_state = normed_one * attn_gain.astype(jnp.float32) + attn_shift.astype(jnp.float32)
    mid_half = mid_state.astype(jnp.bfloat16)
    pre_act = jnp.dot(mid_half, up_weight, preferred_element_type=jnp.float32) + up_bias.astype(jnp.float32)
    hidden = gelu_value(pre_act).astype(jnp.bfloat16)
    ffn_sum = mid_state + jnp.dot(hidden, down_weight, preferred_element_type=jnp.float32) + down_bias.astype(jnp.float32)
    normed_two, inverse_two = layer_norm(ffn_sum)
    layer_output = (normed_two * ffn_gain.astype(jnp.float32) + ffn_shift.astype(jnp.float32)).astype(jnp.bfloat16)
    upstream = cotangent.astype(jnp.float32)
    grad_ffn_shift = lax.optimization_barrier(jnp.sum(upstream, axis=0))
    grad_ffn_gain = lax.optimization_barrier(jnp.sum(upstream * normed_two, axis=0))
    grad_ffn_sum = norm_backward(upstream, normed_two, inverse_two, ffn_gain.astype(jnp.float32))
    ffn_half = grad_ffn_sum.astype(jnp.bfloat16)
    grad_down_weight = jnp.dot(hidden.T, ffn_half, preferred_element_type=jnp.float32)
    grad_down_bias = lax.optimization_barrier(jnp.sum(grad_ffn_sum, axis=0))
    grad_pre = jnp.dot(ffn_half, down_weight.T, preferred_element_type=jnp.float32) * gelu_slope(pre_act)
    pre_half = grad_pre.astype(jnp.bfloat16)
    grad_up_weight = jnp.dot(mid_half.T, pre_half, preferred_element_type=jnp.float32)
    grad_up_bias = lax.optimization_barrier(jnp.sum(grad_pre, axis=0))
    grad_mid = grad_ffn_sum + jnp.dot(pre_half, up_weight.T, preferred_element_type=jnp.float32)
    grad_attn_shift = lax.optimization_barrier(jnp.sum(grad_mid, axis=0))
    grad_attn_gain = lax.optimization_barrier(jnp.sum(grad_mid * normed_one, axis=0))
    grad_attn_sum = norm_backward(grad_mid, normed_one, inverse_one, attn_gain.astype(jnp.float32))
    attn_half = grad_attn_sum.astype(jnp.bfloat16)
    grad_proj_weight = jnp.dot(context.T, attn_half, preferred_element_type=jnp.float32)
    grad_proj_bias = lax.optimization_barrier(jnp.sum(grad_attn_sum, axis=0))
    grad_context = jnp.dot(attn_half, proj_weight.T, preferred_element_type=jnp.float32).astype(jnp.bfloat16)
    context_heads = split_heads(grad_context)
    grad_value = batched('shqk,sqhd->skhd', shares, context_heads)
    grad_shares = batched('sqhd,skhd->shqk', context_heads, split_heads(value_rows))
    grad_scores = (exact * (grad_shares - lax.optimization_barrier(jnp.sum(exact * grad_shares, axis=-1, keepdims=True))) * HEAD_DIM ** (-0.5)).astype(jnp.bfloat16)
    grad_query = merge_heads(batched('shqk,skhd->sqhd', grad_scores, split_heads(key_rows)))
    grad_key = merge_heads(batched('shqk,sqhd->skhd', grad_scores, split_heads(query_rows)))
    grad_value = merge_heads(grad_value)
    grad_query_bias = lax.optimization_barrier(jnp.sum(grad_query, axis=0))
    grad_value_bias = lax.optimization_barrier(jnp.sum(grad_value, axis=0))
    grad_packed = jnp.concatenate([grad_query, grad_key, grad_value], axis=1).astype(jnp.bfloat16)
    grad_qkv_weight = jnp.dot(tokens.T, grad_packed, preferred_element_type=jnp.float32)
    grad_tokens = (grad_attn_sum + jnp.dot(grad_packed, qkv_weight.T, preferred_element_type=jnp.float32)).astype(jnp.bfloat16)
    grads = (grad_qkv_weight, grad_query_bias, grad_value_bias, grad_proj_weight, grad_proj_bias, grad_attn_gain, grad_attn_shift, grad_up_weight, grad_up_bias, grad_down_weight, grad_down_bias, grad_ffn_gain, grad_ffn_shift)
    return (layer_output, grad_tokens, grads)

def reference(tokens, lengths, qkv_weight, query_bias, value_bias, proj_weight, proj_bias, attn_gain, attn_shift, up_weight, up_bias, down_weight, down_bias, ffn_gain, ffn_shift, cotangent):
    params = (qkv_weight, query_bias, value_bias, proj_weight, proj_bias, attn_gain, attn_shift, up_weight, up_bias, down_weight, down_bias, ffn_gain, ffn_shift)
    block_seqs = math.gcd(SEQS, 32)
    block_count = SEQS // block_seqs
    block_rows = block_seqs * LEN

    def one_block(totals, index):
        row_start = (index * block_rows).astype(jnp.int32)
        seq_start = (index * block_seqs).astype(jnp.int32)
        token_block = lax.dynamic_slice_in_dim(tokens, row_start, block_rows, 0)
        length_block = lax.dynamic_slice_in_dim(lengths, seq_start, block_seqs, 0)
        upstream_block = lax.dynamic_slice_in_dim(cotangent, row_start, block_rows, 0)
        output_block, grad_block, grads = layer_pass(token_block, length_block, upstream_block, params)
        return (jax.tree.map(jnp.add, totals, grads), (output_block, grad_block))
    zeros = tuple((jnp.zeros(param.shape, jnp.float32) for param in params))
    totals, (outputs, grads_in) = lax.scan(one_block, zeros, jnp.arange(block_count, dtype=jnp.int32))
    layer_output = outputs.reshape(TOKENS, D)
    grad_tokens = grads_in.reshape(TOKENS, D)
    return (layer_output, grad_tokens, totals[0], totals[1], totals[2], totals[3], totals[4], totals[5], totals[6], totals[7], totals[8], totals[9], totals[10], totals[11], totals[12])
```

```python
import jax
import jax.numpy as jnp
from jax import lax
from jax.sharding import PartitionSpec as P

HEADS = 16
HEAD_DIM = 64
LEN = 128


EPSILON = 1e-05
SQRT_HALF = 0.7071067811865476
INV_ROOT_TAU = 0.3989422804014327

CORE = 1
CHUNK_BYTES = 1 << 20


def gelu_value(pre_act):
    return 0.5 * pre_act * (1.0 + lax.erf(pre_act * SQRT_HALF))


def gelu_slope(pre_act):
    return 0.5 * (1.0 + lax.erf(pre_act * SQRT_HALF)) + pre_act * INV_ROOT_TAU * jnp.exp(
        -0.5 * pre_act * pre_act
    )


def layer_norm(hidden):
    centred = hidden - jnp.mean(hidden, axis=-1, keepdims=True)
    inverse = lax.rsqrt(jnp.mean(centred * centred, axis=-1, keepdims=True) + EPSILON)
    return (centred * inverse, inverse)


def norm_backward(upstream, normed, inverse, gain):
    scaled = upstream * gain
    return inverse * (
        scaled
        - jnp.mean(scaled, axis=-1, keepdims=True)
        - normed * jnp.mean(scaled * normed, axis=-1, keepdims=True)
    )


def contract_rows(former, latter):
    return lax.dot_general(
        former, latter, (((0,), (0,)), ((), ())), preferred_element_type=jnp.float32
    )


def times_transposed(former, latter):
    return lax.dot_general(
        former, latter, (((1,), (1,)), ((), ())), preferred_element_type=jnp.float32
    )


def split_heads(matrix):
    return matrix.reshape(matrix.shape[0] // LEN, LEN, HEADS, HEAD_DIM)


def merge_heads(tensor):
    return tensor.reshape(tensor.shape[0] * LEN, HEADS * HEAD_DIM)


def score_block(query_rows, key_rows, lengths):
    scores = jnp.einsum(
        "sqhd,skhd->shqk",
        split_heads(query_rows),
        split_heads(key_rows),
        preferred_element_type=jnp.float32,
    ) * HEAD_DIM ** (-0.5)
    positions = jnp.arange(LEN, dtype=jnp.int32)
    usable = (positions[None, :] < lengths[:, None])[:, None, None, :]
    return (scores, usable)


def attention_backward(query_rows, key_rows, value_rows, log_total, lengths, grad_context):
    scores, usable = score_block(query_rows, key_rows, lengths)
    exact = jnp.where(usable, jnp.exp(scores - log_total), 0.0)
    shares = exact.astype(jnp.bfloat16)
    context_heads = split_heads(grad_context)
    grad_value = jnp.einsum(
        "shqk,sqhd->skhd", shares, context_heads, preferred_element_type=jnp.float32
    )
    grad_shares = jnp.einsum(
        "sqhd,skhd->shqk",
        context_heads,
        split_heads(value_rows),
        preferred_element_type=jnp.float32,
    )
    grad_scores = (
        exact
        * (grad_shares - jnp.sum(exact * grad_shares, axis=-1, keepdims=True))
        * HEAD_DIM ** (-0.5)
    ).astype(jnp.bfloat16)
    grad_query = jnp.einsum(
        "shqk,skhd->sqhd", grad_scores, split_heads(key_rows), preferred_element_type=jnp.float32
    )
    grad_key = jnp.einsum(
        "shqk,sqhd->skhd", grad_scores, split_heads(query_rows), preferred_element_type=jnp.float32
    )
    return (merge_heads(grad_query), merge_heads(grad_key), merge_heads(grad_value))


class Links:
    def __init__(self, reps, shards):
        self.reps, self.shards = reps, shards
        self.rep = lax.axis_index("rep")
        self.shard = lax.axis_index("shard")
        self.core = self.rep % 2
        self.bits = [1 << j for j in range(1, reps.bit_length() - 1)]

    def swap(self, value, rep_mask=0, shard_mask=0):
        mask = rep_mask * self.shards + shard_mask
        pairs = [(i, i ^ mask) for i in range(self.reps * self.shards)]
        return lax.ppermute(value, ("rep", "shard"), pairs)

    def bit(self, mask):
        return (self.rep // mask) % 2

    def gather_rows(self, weight, turn):
        rows = weight.shape[0]
        full = jnp.concatenate([weight] * self.shards, axis=0)
        chunks = 1 << (max(1, weight.size * 2 // CHUNK_BYTES).bit_length() - 1)
        step = rows // chunks
        for i in range(chunks):
            masks = (self.bits[(turn + i) % 2], CORE) if len(self.bits) > 1 else (CORE,)
            size = step >> len(masks)
            mine = sum(self.bit(b) << j for j, b in enumerate(masks))
            piece = lax.dynamic_slice_in_dim(weight, i * step + mine * size, size)
            for other in range(1, self.shards):
                got = {0: self.swap(piece, 0, other)}
                for j, b in enumerate(masks):
                    got.update({k ^ (1 << j): self.swap(v, b) for k, v in list(got.items())})
                for k, v in got.items():
                    at = (self.shard ^ other) * rows + i * step + (mine ^ k) * size
                    full = lax.dynamic_update_slice_in_dim(full, v, at, 0)
        return full

    def gather_vectors(self, vectors):
        packed = jnp.concatenate(vectors)[None]
        full = jnp.concatenate([packed] * self.shards, axis=0)
        for other in range(1, self.shards):
            full = lax.dynamic_update_slice_in_dim(
                full, self.swap(packed, 0, other), self.shard ^ other, 0
            )
        out, at = [], 0
        for v in vectors:
            out.append(full[:, at : at + v.size].reshape(-1).astype(jnp.float32))
            at += v.size
        return out

    def group_columns(self, value):
        width = value.shape[1] // self.shards
        own = [lax.dynamic_slice_in_dim(value, self.shard * width, width, 1)]
        for other in range(1, self.shards):
            sent = lax.dynamic_slice_in_dim(value, (self.shard ^ other) * width, width, 1)
            own.append(self.swap(sent, 0, other))
        return jnp.concatenate(own + [self.swap(v, CORE) for v in own], axis=0)

    def group_half(self, value):
        width = value.shape[1] // 2
        own = lax.dynamic_slice_in_dim(value, self.core * width, width, 1)
        twin = self.swap(lax.dynamic_slice_in_dim(value, (1 - self.core) * width, width, 1), CORE)
        return jnp.concatenate(
            [own]
            + [self.swap(own, 0, other) for other in range(1, self.shards)]
            + [twin]
            + [self.swap(twin, 0, other) for other in range(1, self.shards)],
            axis=0,
        )

    def weight_gradient(self, columns, half):
        rows, width = columns.shape[1], half.shape[1]
        bits = self.bits
        if bits:
            part = rows // 2
            at = self.bit(bits[0])
            sent = contract_rows(
                lax.dynamic_slice_in_dim(columns, (1 - at) * part, part, 1), half
            ).astype(jnp.bfloat16)
            arrived = self.swap(sent, bits[0])
            kept = contract_rows(lax.dynamic_slice_in_dim(columns, at * part, part, 1), half)
            total = (kept + arrived.astype(jnp.float32)).astype(jnp.bfloat16)
        else:
            total = contract_rows(columns, half).astype(jnp.bfloat16)
        for b in bits[1:]:
            part = total.shape[0] // 2
            at = self.bit(b)
            arrived = self.swap(lax.dynamic_slice_in_dim(total, (1 - at) * part, part), b)
            kept = lax.dynamic_slice_in_dim(total, at * part, part)
            total = (kept.astype(jnp.float32) + arrived.astype(jnp.float32)).astype(jnp.bfloat16)
        for b in bits[:0:-1]:
            arrived = self.swap(total, b)
            total = jnp.where(
                self.bit(b) == 0,
                jnp.concatenate([total, arrived]),
                jnp.concatenate([arrived, total]),
            )
        whole = jnp.zeros((rows, 2 * width), jnp.float32)
        blocks = [(total, 0, self.core)]
        if bits:
            at = self.bit(bits[0])
            part = total.shape[0]
            blocks = [(total, at * part, self.core), (self.swap(total, bits[0]), (1 - at) * part, self.core)]
        blocks += [(self.swap(v, CORE), row, 1 - self.core) for v, row, _ in blocks]
        for v, row, side in blocks:
            whole = lax.dynamic_update_slice(whole, v.astype(jnp.float32), (row, side * width))
        return whole

    def sum_vectors(self, vectors):
        packed = jnp.concatenate([v.reshape(self.shards, -1) for v in vectors], axis=1)
        total = lax.dynamic_slice_in_dim(packed, self.shard, 1)
        for other in range(1, self.shards):
            total = total + self.swap(
                lax.dynamic_slice_in_dim(packed, self.shard ^ other, 1), 0, other
            )
        for b in [CORE] + self.bits:
            total = total + self.swap(total, b)
        out, at = [], 0
        for v in vectors:
            size = v.size // self.shards
            out.append(total[0, at : at + size])
            at += size
        return out


def per_device(
    reps,
    shards,
    tokens,
    lengths,
    qkv_weight,
    query_bias,
    value_bias,
    proj_weight,
    proj_bias,
    attn_gain,
    attn_shift,
    up_weight,
    up_bias,
    down_weight,
    down_bias,
    ffn_gain,
    ffn_shift,
    cotangent,
):
    links = Links(reps, shards)
    (
        query_full,
        value_full,
        proj_bias_full,
        attn_gain_full,
        attn_shift_full,
        up_bias_full,
        down_bias_full,
        ffn_gain_full,
        ffn_shift_full,
    ) = links.gather_vectors(
        [
            query_bias,
            value_bias,
            proj_bias,
            attn_gain,
            attn_shift,
            up_bias,
            down_bias,
            ffn_gain,
            ffn_shift,
        ]
    )
    qkv_full = links.gather_rows(qkv_weight, 0)
    proj_full = links.gather_rows(proj_weight, 1)
    up_full = links.gather_rows(up_weight, 0)
    down_full = links.gather_rows(down_weight, 0)

    model_width = tokens.shape[1]
    project = jnp.dot(tokens, qkv_full, preferred_element_type=jnp.float32)
    query_rows = (project[:, :model_width] + query_full).astype(jnp.bfloat16)
    key_rows = project[:, model_width : 2 * model_width].astype(jnp.bfloat16)
    value_rows = (project[:, 2 * model_width :] + value_full).astype(jnp.bfloat16)
    scores, usable = score_block(query_rows, key_rows, lengths)
    log_total = jnp.log(jnp.sum(jnp.where(usable, jnp.exp(scores), 0.0), axis=-1, keepdims=True))
    shares = jnp.where(usable, jnp.exp(scores - log_total), 0.0).astype(jnp.bfloat16)
    context = merge_heads(
        jnp.einsum(
            "shqk,skhd->sqhd", shares, split_heads(value_rows), preferred_element_type=jnp.float32
        )
    ).astype(jnp.bfloat16)
    attn_sum = (
        tokens.astype(jnp.float32)
        + jnp.dot(context, proj_full, preferred_element_type=jnp.float32)
        + proj_bias_full
    )
    normed_one, inverse_one = layer_norm(attn_sum)
    mid_state = normed_one * attn_gain_full + attn_shift_full
    mid_half = mid_state.astype(jnp.bfloat16)
    pre_act = jnp.dot(mid_half, up_full, preferred_element_type=jnp.float32) + up_bias_full
    hidden = gelu_value(pre_act).astype(jnp.bfloat16)
    ffn_sum = (
        mid_state + jnp.dot(hidden, down_full, preferred_element_type=jnp.float32) + down_bias_full
    )
    normed_two, inverse_two = layer_norm(ffn_sum)
    layer_output = (normed_two * ffn_gain_full + ffn_shift_full).astype(jnp.bfloat16)
    token_cols = links.group_columns(tokens)
    context_cols = links.group_columns(context)
    mid_cols = links.group_columns(mid_half)
    hidden_cols = links.group_columns(hidden)
    upstream = cotangent.astype(jnp.float32)
    grad_ffn_shift = jnp.sum(upstream, axis=0)
    grad_ffn_gain = jnp.sum(upstream * normed_two, axis=0)
    grad_ffn_sum = norm_backward(upstream, normed_two, inverse_two, ffn_gain_full)
    ffn_half = grad_ffn_sum.astype(jnp.bfloat16)
    grad_down_bias = jnp.sum(grad_ffn_sum, axis=0)
    grad_down_weight = links.weight_gradient(hidden_cols, links.group_half(ffn_half))
    grad_pre = times_transposed(ffn_half, down_full) * gelu_slope(pre_act)
    pre_half = grad_pre.astype(jnp.bfloat16)
    grad_up_bias = jnp.sum(grad_pre, axis=0)
    grad_up_weight = links.weight_gradient(mid_cols, links.group_half(pre_half))
    grad_mid = grad_ffn_sum + times_transposed(pre_half, up_full)
    grad_attn_shift = jnp.sum(grad_mid, axis=0)
    grad_attn_gain = jnp.sum(grad_mid * normed_one, axis=0)
    grad_attn_sum = norm_backward(grad_mid, normed_one, inverse_one, attn_gain_full)
    attn_half = grad_attn_sum.astype(jnp.bfloat16)
    grad_proj_bias = jnp.sum(grad_attn_sum, axis=0)
    grad_proj_weight = links.weight_gradient(context_cols, links.group_half(attn_half))
    grad_context = times_transposed(attn_half, proj_full).astype(jnp.bfloat16)
    grad_query, grad_key, grad_value = attention_backward(
        query_rows, key_rows, value_rows, log_total, lengths, grad_context
    )
    grad_query_bias = jnp.sum(grad_query, axis=0)
    grad_value_bias = jnp.sum(grad_value, axis=0)
    grad_packed = jnp.concatenate([grad_query, grad_key, grad_value], axis=1).astype(jnp.bfloat16)
    grad_qkv_weight = links.weight_gradient(token_cols, links.group_half(grad_packed))
    grad_tokens = (grad_attn_sum + times_transposed(grad_packed, qkv_full)).astype(jnp.bfloat16)
    (
        grad_query_bias,
        grad_value_bias,
        grad_proj_bias,
        grad_attn_gain,
        grad_attn_shift,
        grad_up_bias,
        grad_down_bias,
        grad_ffn_gain,
        grad_ffn_shift,
    ) = links.sum_vectors(
        [
            grad_query_bias,
            grad_value_bias,
            grad_proj_bias,
            grad_attn_gain,
            grad_attn_shift,
            grad_up_bias,
            grad_down_bias,
            grad_ffn_gain,
            grad_ffn_shift,
        ]
    )
    return (
        layer_output,
        grad_tokens,
        grad_qkv_weight,
        grad_query_bias,
        grad_value_bias,
        grad_proj_weight,
        grad_proj_bias,
        grad_attn_gain,
        grad_attn_shift,
        grad_up_weight,
        grad_up_bias,
        grad_down_weight,
        grad_down_bias,
        grad_ffn_gain,
        grad_ffn_shift,
    )


def solution(mesh):
    reps, shards = mesh.shape["rep"], mesh.shape["shard"]
    assert reps & (reps - 1) == 0 and shards & (shards - 1) == 0 and reps > 1

    def body(*args):
        return per_device(reps, shards, *args)

    rows, row, vec = P(("rep", "shard"), None), P("shard", None), P("shard")
    return jax.shard_map(
        body,
        mesh=mesh,
        in_specs=(
            rows,
            P(("rep", "shard")),
            row,
            vec,
            vec,
            row,
            vec,
            vec,
            vec,
            row,
            vec,
            row,
            vec,
            vec,
            vec,
            rows,
        ),
        out_specs=(
            rows,
            rows,
            row,
            vec,
            vec,
            row,
            vec,
            vec,
            vec,
            row,
            vec,
            row,
            vec,
            vec,
            vec,
        ),
        check_vma=False,
    )
```
